32 devices in a mesh: grp: 2 (over y), mk: 4 (over z), pp: 2 (over x), sub: 2 (over core).
Axes of the slice: x: 2, y: 2, z: 4, core: 2. Of those that a mesh axis runs over, the one named last changes fastest.
Arguments:
- genotypes: bfloat16 [4096, 16384], P(('grp', 'pp', 'sub'), 'mk'), parts along dimension 0, may hold values from -6 to 6
- estimate: bfloat16 [512, 16384], P(('grp', 'pp', 'sub'), 'mk'), parts along dimension 0, may hold values from -0.046875 to 0.046875
- phenotypes: bfloat16 [512, 2048], P('grp', ('pp', 'sub')), parts along dimension 0, may hold values from -6 to 6
- prior_logit: float32 [512], P(('grp', 'pp', 'sub')), parts along dimension 0, may hold values from -2 to 1
- slab_var: float32 [512], P(('grp', 'pp', 'sub')), parts along dimension 0, may hold values from 0.5 to 4
- noise_var: float32 [512], P(('grp', 'pp', 'sub')), parts along dimension 0, may hold values from 0.5 to 2
- tile_chrom: int32 [64], P('grp'), parts along dimension 0, may hold values from 0 to 21, as said below
Outputs:
- updated: bfloat16 [512, 16384], P(('grp', 'pp', 'sub'), 'mk'), parts along dimension 0
- loco_out: bfloat16 [44, 256, 2048], P('grp', 'mk', ('pp', 'sub')), parts along dimension 0
The draws below stay inside these ranges and needn't reach their ends.
There are 2 independent parts, one for each index of `grp`. The reference program is written for one: setup_inputs(seed, part) draws one part's arguments, and reference() takes and returns one part's arrays. A program takes and returns all parts, laid end to end along the dimension named above; each array names one. Nothing has to cross between parts.
Inputs may be any that keep to these rules, and one draw needn't show every extreme that they name: `tile_chrom`: never falling along the tiles; every chromosome owns at least one tile; the tiles of one device (aligned blocks of 8 tiles) name at most 6 chromosomes, and some device names exactly 6.
All inputs are finite; a program needn't handle non-finite values.
Results may differ from the reference program's by a relative error of at most 0.0059.
Values may be sent and summed in bfloat16 or wider, within the bound.
A program may use at most 64 MiB of HBM per device.

```python
import math
import jax
import jax.numpy as jnp
from jax import lax

TRAITS = 256
CHROMS = 22
TILE = 512
SPAN = 6
MARK_DEV = 4096
PEOPLE = 2048
MARKERS = 16384
TILES = 32
N_MK = 4


def draw_tile_chrom(key, part):
    tile_dev = MARK_DEV // TILE
    place_count = TILES - 1
    subkeys = jax.random.split(key, 2)
    scores = jax.random.permutation(subkeys[0], place_count).astype(jnp.int32)
    places = jnp.arange(1, TILES, dtype=jnp.int32)
    owners = places // tile_dev
    inside = places % tile_dev != 0
    same_dev = (owners[:, None] == owners[None, :]) & inside[None, :] & inside[:, None]
    higher = jnp.sum((same_dev & (scores[None, :] > scores[:, None])).astype(jnp.int32), axis=1)
    allowed = jnp.logical_not(inside) | (higher < SPAN - 1)
    chosen_dev = jax.random.randint(subkeys[1], (), 0, N_MK).astype(jnp.int32)
    forced = inside & (owners == chosen_dev) & (higher < SPAN - 1)
    priority = jnp.where(forced, scores + 2 * TILES, jnp.where(allowed, scores, -TILES - places))
    top_values, picked = lax.top_k(priority, CHROMS - 1)
    increments = jnp.zeros((place_count,), jnp.int32).at[picked].set(1)
    return jnp.concatenate([jnp.zeros((1,), jnp.int32), jnp.cumsum(increments).astype(jnp.int32)])


def block_scale(key, shape, cuts, least, high):
    level, own = 1.0, jax.random.fold_in(key, 6)
    for axis_at, shards_of in cuts:
        heights = jnp.exp(jax.random.uniform(jax.random.fold_in(own, axis_at), (shards_of,), jnp.float32, least / len(cuts), high / len(cuts)))
        level = level * jnp.repeat(heights, shape[axis_at] // shards_of).reshape([-1 if axis == axis_at else 1 for axis in range(len(shape))])
    return level


def normal_values(stream_key, extent, scale, limit, shards=(), kind=jnp.bfloat16):
    level = block_scale(stream_key, extent, shards, -0.22, 0.18) if shards else 1.0
    drawn = jax.random.normal(stream_key, extent, jnp.float32) * scale * level
    return jnp.minimum(jnp.maximum(drawn, -limit), limit).astype(kind)


def setup_inputs(seed: int = 0, part: int = 0) -> dict:
    keys = jax.random.split(jax.random.key(seed), 8)
    part_splits = jax.random.split(jax.random.fold_in(keys[7], part), 8)
    return {
        "genotypes": normal_values(part_splits[0], (PEOPLE, MARKERS), 1.0, 6.0, ((0, 4), (1, 4))),
        "estimate": normal_values(part_splits[1], (TRAITS, MARKERS), MARKERS ** -0.5, 0.046875, ((0, 4), (1, 4))),
        "phenotypes": normal_values(part_splits[2], (TRAITS, PEOPLE), 1.0, 6.0, ((1, 4),)),
        "prior_logit": jnp.clip(-2.0 + 3.0 * jax.random.uniform(part_splits[3], (TRAITS,), jnp.float32) ** block_scale(part_splits[3], (TRAITS,), ((0, 4),), -0.2, 0.2), -2.0, 1.0),
        "slab_var": jnp.clip(jnp.exp(math.log(4.0) - 2.0794415 * jax.random.uniform(part_splits[4], (TRAITS,), jnp.float32) ** block_scale(part_splits[4], (TRAITS,), ((0, 4),), -0.2, 0.2)), 0.5, 4.0),
        "noise_var": jnp.clip(jnp.exp(math.log(2.0) - 1.3862944 * jax.random.uniform(part_splits[5], (TRAITS,), jnp.float32) ** block_scale(part_splits[5], (TRAITS,), ((0, 4),), -0.2, 0.2)), 0.5, 2.0),
        "tile_chrom": draw_tile_chrom(jax.random.fold_in(jax.random.fold_in(keys[7], part), 71), part),
    }


def denoise(estimate, scores, prior_logit, slab_var, noise_var, marker_root, people_root):
    observed = marker_root * estimate.astype(jnp.float32) + scores * (1.0 / people_root)
    slab_col = slab_var[:, None]
    noise_col = noise_var[:, None]
    spread = slab_col + noise_col
    log_odds = prior_logit[:, None] + 0.5 * jnp.log(noise_col / spread) + 0.5 * observed * observed * (1.0 / noise_col - 1.0 / spread)
    posterior = jax.nn.sigmoid(log_odds) * (slab_col / spread) * observed
    return (posterior * (1.0 / marker_root)).astype(jnp.bfloat16)

def reference(genotypes, estimate, phenotypes, prior_logit, slab_var, noise_var, tile_chrom):
    prediction = lax.dot_general(estimate, genotypes, (((1,), (1,)), ((), ())), preferred_element_type=jnp.float32)
    residual = (phenotypes.astype(jnp.float32) - prediction).astype(jnp.bfloat16)
    scores = jnp.dot(residual, genotypes, preferred_element_type=jnp.float32)
    updated = denoise(estimate, scores, prior_logit, slab_var, noise_var, math.sqrt(MARKERS), math.sqrt(PEOPLE))

    def add_tile(tile_index, buffer):
        where_at = (tile_index * TILE).astype(jnp.int32)
        geno_tile = lax.dynamic_slice_in_dim(genotypes, where_at, TILE, 1)
        est_tile = lax.dynamic_slice_in_dim(updated, where_at, TILE, 1)
        product = lax.dot_general(est_tile, geno_tile, (((1,), (1,)), ((), ())), preferred_element_type=jnp.float32)
        chrom_id = lax.dynamic_index_in_dim(tile_chrom, tile_index.astype(jnp.int32), 0, keepdims=False).astype(jnp.int32)
        old_row = lax.dynamic_index_in_dim(buffer, chrom_id, 0, keepdims=False)
        return lax.dynamic_update_index_in_dim(buffer, old_row + product, chrom_id, 0)
    chrom_sums = lax.fori_loop(0, TILES, add_tile, jnp.zeros((CHROMS, TRAITS, PEOPLE), jnp.float32))
    combined = lax.optimization_barrier(jnp.sum(chrom_sums, axis=0))
    loco_out = (phenotypes.astype(jnp.float32)[None] - combined[None] + chrom_sums).astype(jnp.bfloat16)
    return (updated, loco_out)
```

```python
import functools
import math

import jax
import jax.numpy as jnp
from jax import lax
from jax.experimental import pallas as pl
from jax.experimental.pallas import tpu as pltpu
from jax.sharding import PartitionSpec as P

CHROMS = 22
TILE = 512
SPAN = 6
CHUNKS = 4
F32 = jnp.float32
BF16 = jnp.bfloat16
NT = (((1,), (1,)), ((), ()))


def column(row):
    n = row.shape[1]
    at = lax.broadcasted_iota(jnp.int32, (n, n), 0)
    to = lax.broadcasted_iota(jnp.int32, (n, n), 1)
    return jnp.sum(jnp.where(at == to, jnp.broadcast_to(row, (n, n)), 0.0), axis=1, keepdims=True)


def kernel(dims, tc_ref, geno_hbm, est_hbm, phen_ref, prior_ref, slab_ref, noise_ref,
           upd_ref, loco_ref,
           geno, estbuf, pown, pbuf, precv, rbuf, sbuf, c1send, c1recv, c2send, c2recv,
           ubuf, tbuf, ebuf,
           lsem, ax_s, ax_r, ap_s, ap_r, bz_s, bz_r, rz_s, rz_r, c1_s, c1_r, c2_s, c2_r,
           dx_s, dx_r, dp_s, dp_r, ez_s, ez_r, *erecv):
    n_mk, n_pp, chunks, rows, rb, share, g, people, marks, marker_root, people_root = dims
    n_sh = n_pp * 2
    tile_dev = marks // TILE
    x, s, z = lax.axis_index("pp"), lax.axis_index("sub"), lax.axis_index("mk")
    other = 1 - s
    me = x * 2 + s
    partner = {"sub": other}

    def xid(d):
        return lax.rem(x + d, n_pp)

    def xback(d):
        return lax.rem(x + n_pp - d, n_pp)

    def zid(d):
        return lax.rem(z + d, n_mk)

    def remote(src, dst, send, recv, where):
        return pltpu.make_async_remote_copy(
            src_ref=src, dst_ref=dst, send_sem=send, recv_sem=recv,
            device_id=where, device_id_type=pl.DeviceIdType.MESH)

    started = []

    def go(copy):
        copy.start()
        started.append(copy)
        return copy

    load_geno = pltpu.make_async_copy(geno_hbm, geno, lsem.at[0])
    load_geno.start()
    own_loads = []
    for c in range(chunks):
        own = pltpu.make_async_copy(est_hbm.at[pl.ds(c * rb, rb)], estbuf.at[c, me], lsem.at[1 + c])
        own.start()
        own_loads.append(own)

    barrier = pltpu.get_barrier_semaphore()
    peers = [partner] + [{"pp": xid(d)} for d in range(1, n_pp)] + [{"mk": zid(d)} for d in range(1, n_mk)]
    for peer in peers:
        pl.semaphore_signal(barrier, inc=1, device_id=peer, device_id_type=pl.DeviceIdType.MESH)
    pl.semaphore_wait(barrier, len(peers))

    copies = {}

    def gather_start(kind, c, src, buf, xs, xr, ps, pr):
        copies[kind, c, "x"] = [
            go(remote(src, buf.at[c, me], xs.at[c, d - 1], xr.at[c, d - 1], {"pp": xid(d)}))
            for d in range(1, n_pp)]
        copies[kind, c, "p"] = [go(remote(src, buf.at[c, me], ps.at[c, 0], pr.at[c, 0], partner))]

    def gather_forward(kind, c, buf, ps, pr):
        for d in range(1, n_pp):
            copies[kind, c, "x"][d - 1].wait_recv()
            origin = xback(d) * 2 + s
            copies[kind, c, "p"].append(
                go(remote(buf.at[c, origin], buf.at[c, origin], ps.at[c, d], pr.at[c, d], partner)))

    def gather_finish(kind, c):
        for copy in copies[kind, c, "p"]:
            copy.wait_recv()

    slab, noise = column(slab_ref[...]), column(noise_ref[...])
    spread = slab + noise
    base = column(prior_ref[...]) + 0.5 * jnp.log(noise / spread)
    curve = 1.0 / noise - 1.0 / spread
    shrink = slab / spread

    first = tc_ref[z * tile_dev]
    member = [[jnp.where(tc_ref[z * tile_dev + t] == first + k, 1.0, 0.0).astype(F32)
               for t in range(tile_dev)] for k in range(SPAN)]

    def a0(c):
        gather_start("a", c, est_hbm.at[pl.ds(c * rb, rb)], estbuf, ax_s, ax_r, ap_s, ap_r)

    def a1(c):
        gather_forward("a", c, estbuf, ap_s, ap_r)

    def a2(c):
        if c == 0:
            load_geno.wait()
        own_loads[c].wait()
        gather_finish("a", c)
        pred = lax.dot_general(estbuf[c].reshape(n_sh * rb, marks), geno[...], NT,
                               preferred_element_type=F32)
        pown[c] = pred.reshape(n_mk, g, people)
        pbuf[c] = pred.astype(BF16).reshape(n_mk, g, people)
        copies["b", c] = [
            go(remote(pbuf.at[c, zid(d)], precv.at[c, d - 1], bz_s.at[c, d - 1], bz_r.at[c, d - 1], {"mk": zid(d)}))
            for d in range(1, n_mk)]

    def phen_rows(c):
        return phen_ref[pl.ds(pl.multiple_of(z * share + c * g, g), g), :].astype(F32)

    def b1(c):
        total = pown[c, z]
        for d in range(1, n_mk):
            copies["b", c][d - 1].wait_recv()
            total = total + precv[c, d - 1].astype(F32)
        rbuf[c, z] = (phen_rows(c) - total).astype(BF16)
        copies["r", c] = [
            go(remote(rbuf.at[c, z], rbuf.at[c, z], rz_s.at[c, d - 1], rz_r.at[c, d - 1], {"mk": zid(d)}))
            for d in range(1, n_mk)]

    def b2(c):
        for copy in copies["r", c]:
            copy.wait_recv()
        residual = rbuf[c].reshape(n_sh * rb, people)
        for j in range(marks // TILE):
            cols = pl.ds(j * TILE, TILE)
            sbuf[c, :, :, cols] = jnp.dot(residual, geno[:, cols], preferred_element_type=F32).reshape(n_sh, rb, TILE)
        for q in range(n_pp):
            c1send[c, q] = sbuf[c, q * 2 + other].astype(BF16)
        copies["c1", c] = go(remote(c1send.at[c], c1recv.at[c], c1_s.at[c], c1_r.at[c], partner))

    def c2(c):
        copies["c1", c].wait_recv()
        copies["c2", c] = []
        for d in range(1, n_pp):
            q = xid(d)
            c2send[c, d - 1] = (sbuf[c, q * 2 + s] + c1recv[c, q].astype(F32)).astype(BF16)
            copies["c2", c].append(
                go(remote(c2send.at[c, d - 1], c2recv.at[c, d - 1], c2_s.at[c, d - 1], c2_r.at[c, d - 1], {"pp": q})))

    def c3(c):
        for copy in copies["c2", c]:
            copy.wait_recv()
        at = slice(c * rb, (c + 1) * rb)
        scores = sbuf[c, me] + c1recv[c, x].astype(F32)
        for d in range(1, n_pp):
            scores = scores + c2recv[c, d - 1].astype(F32)
        observed = marker_root * estbuf[c, me].astype(F32) + scores * (1.0 / people_root)
        log_odds = base[at] + 0.5 * observed * observed * curve[at]
        posterior = jax.nn.sigmoid(log_odds) * shrink[at] * observed
        new = (posterior * (1.0 / marker_root)).astype(BF16)
        ubuf[c, me] = new
        upd_ref[at, :] = new
        gather_start("d", c, ubuf.at[c, me], ubuf, dx_s, dx_r, dp_s, dp_r)

    def d1(c):
        gather_forward("d", c, ubuf, dp_s, dp_r)

    def d2(c):
        gather_finish("d", c)
        for t in range(tile_dev):
            cols = pl.ds(t * TILE, TILE)
            tbuf[t] = lax.dot_general(ubuf[c, :, :, cols].reshape(n_sh * rb, TILE), geno[:, cols], NT,
                                      preferred_element_type=F32).reshape(n_mk, g, people)
        for b in range(n_mk):
            for k in range(SPAN):
                acc = tbuf[0, b] * member[k][0]
                for t in range(1, tile_dev):
                    acc = acc + tbuf[t, b] * member[k][t]
                ebuf[c, b, k] = acc.astype(BF16)
        copies["e", c] = [
            go(remote(ebuf.at[c, zid(d)], erecv[c].at[d - 1], ez_s.at[c, d - 1], ez_r.at[c, d - 1], {"mk": zid(d)}))
            for d in range(1, n_mk)]

    def e1(c):
        for copy in copies["e", c]:
            copy.wait_recv()
        total = jnp.zeros((g, people), F32)
        for k in range(SPAN):
            total = total + ebuf[c, z, k].astype(F32)
            for d in range(1, n_mk):
                total = total + erecv[c][d - 1, k].astype(F32)
        rest = phen_rows(c) - total
        for q in range(CHROMS):
            value = rest
            for d in range(n_mk):
                source = lax.rem(z + n_mk - d, n_mk)
                slot = q - tc_ref[source * tile_dev]
                held = jnp.where((slot >= 0) & (slot < SPAN), 1.0, 0.0).astype(F32)
                slot = jnp.clip(slot, 0, SPAN - 1)
                block = ebuf[c, z, slot] if d == 0 else erecv[c][d - 1, slot]
                value = value + block.astype(F32) * held
            loco_ref[q, c * g:(c + 1) * g, :] = value.astype(BF16)

    stages = [a1, a2, b1, b2, c2, c3, d1, d2, e1]
    for c in range(chunks):
        a0(c)
    for step in range(len(stages) + chunks - 1):
        for c in range(chunks):
            if 0 <= step - c < len(stages):
                stages[step - c](c)
    for copy in started:
        copy.wait_send()


def per_device(genotypes, estimate, phenotypes, prior_logit, slab_var, noise_var, tile_chrom):
    people, marks = genotypes.shape
    n_mk, n_pp, n_sub = lax.axis_size("mk"), lax.axis_size("pp"), lax.axis_size("sub")
    traits, rows = phenotypes.shape[0], estimate.shape[0]
    share = traits // n_mk
    assert n_sub == 2
    chunks = CHUNKS if share == rows and rows % (16 * CHUNKS) == 0 else 1
    rb, g = rows // chunks, share // chunks
    n_sh, tile_dev = n_pp * 2, marks // TILE
    dims = (n_mk, n_pp, chunks, rows, rb, share, g, people, marks,
            math.sqrt(marks * n_mk), math.sqrt(people * n_pp * n_sub))
    vmem, dma = pltpu.VMEM, pltpu.SemaphoreType.DMA
    xs, zs = n_pp - 1, n_mk - 1
    in_vmem = pl.BlockSpec(memory_space=pltpu.VMEM)
    in_any = pl.BlockSpec(memory_space=pl.ANY)
    return pl.pallas_call(
        functools.partial(kernel, dims),
        out_shape=(jax.ShapeDtypeStruct((rows, marks), BF16),
                   jax.ShapeDtypeStruct((CHROMS, share, people), BF16)),
        in_specs=[pl.BlockSpec(memory_space=pltpu.SMEM), in_any, in_any, in_vmem, in_vmem, in_vmem, in_vmem],
        out_specs=(in_vmem, in_vmem),
        scratch_shapes=[
            vmem((people, marks), BF16),
            vmem((chunks, n_sh, rb, marks), BF16),
            vmem((chunks, n_mk, g, people), F32),
            vmem((chunks, n_mk, g, people), BF16),
            vmem((chunks, zs, g, people), BF16),
            vmem((chunks, n_mk, g, people), BF16),
            vmem((chunks, n_sh, rb, marks), F32),
            vmem((chunks, n_pp, rb, marks), BF16),
            vmem((chunks, n_pp, rb, marks), BF16),
            vmem((chunks, xs, rb, marks), BF16),
            vmem((chunks, xs, rb, marks), BF16),
            vmem((chunks, n_sh, rb, marks), BF16),
            vmem((tile_dev, n_mk, g, people), F32),
            vmem((chunks, n_mk, SPAN, g, people), BF16),
            dma((1 + chunks,)),
            dma((chunks, xs)), dma((chunks, xs)), dma((chunks, n_pp)), dma((chunks, n_pp)),
            dma((chunks, zs)), dma((chunks, zs)), dma((chunks, zs)), dma((chunks, zs)),
            dma((chunks,)), dma((chunks,)), dma((chunks, xs)), dma((chunks, xs)),
            dma((chunks, xs)), dma((chunks, xs)), dma((chunks, n_pp)), dma((chunks, n_pp)),
            dma((chunks, zs)), dma((chunks, zs)),
        ] + [vmem((zs, SPAN, g, people), BF16) for _ in range(chunks)],
        compiler_params=pltpu.CompilerParams(
            collective_id=0, has_side_effects=True, vmem_limit_bytes=56 * 1024 * 1024),
    )(tile_chrom, genotypes, estimate, phenotypes,
      prior_logit.reshape(1, rows), slab_var.reshape(1, rows), noise_var.reshape(1, rows))


def solution(mesh):
    placed = (
        P(("grp", "pp", "sub"), "mk"),
        P(("grp", "pp", "sub"), "mk"),
        P("grp", ("pp", "sub")),
        P(("grp", "pp", "sub")),
        P(("grp", "pp", "sub")),
        P(("grp", "pp", "sub")),
        P("grp"),
    )
    return jax.shard_map(
        per_device,
        mesh=mesh,
        in_specs=placed,
        out_specs=(P(("grp", "pp", "sub"), "mk"), P("grp", "mk", ("pp", "sub"))),
        check_vma=False,
    )
```

```python
import functools
import math

import jax
import jax.numpy as jnp
from jax import lax
from jax.experimental import pallas as pl
from jax.experimental.pallas import tpu as pltpu
from jax.sharding import PartitionSpec as P

CHROMS = 22
TILE = 512
SPAN = 6
CHUNKS = 4
ORDER = [
    [0, 10, 1, 11, 20, 2, 12, 30, 21, 3, 13, 40, 22, 31, 50, 41, 23, 32],
    [60, 33, 70, 51, 42, 61, 71, 52, 43, 62, 80, 72, 53, 63, 73, 81, 82, 83],
]
F32 = jnp.float32
BF16 = jnp.bfloat16
NT = (((1,), (1,)), ((), ()))


def column(row):
    n = row.shape[1]
    at = lax.broadcasted_iota(jnp.int32, (n, n), 0)
    to = lax.broadcasted_iota(jnp.int32, (n, n), 1)
    return jnp.sum(jnp.where(at == to, jnp.broadcast_to(row, (n, n)), 0.0), axis=1, keepdims=True)


def kernel(dims, tc_ref, geno_hbm, est_hbm, phen_ref, prior_ref, slab_ref, noise_ref,
           upd_hbm, slots_hbm,
           geno, estbuf, pown, pbuf, precv, rbuf, sbuf, c1send, c1recv, c2send, c2recv,
           ubuf, tbuf, ebuf,
           lsem, osem, ksem, ax_s, ax_r, ap_s, ap_r, bz_s, bz_r, rz_s, rz_r, c1_s, c1_r, c2_s, c2_r,
           dx_s, dx_r, dp_s, dp_r, ez_s, ez_r):
    n_mk, n_pp, chunks, rows, rb, share, g, people, marks, marker_root, people_root = dims
    n_sh = n_pp * 2
    tile_dev = marks // TILE
    x, s, z = lax.axis_index("pp"), lax.axis_index("sub"), lax.axis_index("mk")
    other = 1 - s
    me = x * 2 + s
    partner = {"sub": other}

    def xid(d):
        return lax.rem(x + d, n_pp)

    def xback(d):
        return lax.rem(x + n_pp - d, n_pp)

    def zid(d):
        return lax.rem(z + d, n_mk)

    def remote(src, dst, send, recv, where):
        return pltpu.make_async_remote_copy(
            src_ref=src, dst_ref=dst, send_sem=send, recv_sem=recv,
            device_id=where, device_id_type=pl.DeviceIdType.MESH)

    started = []

    def go(copy):
        copy.start()
        started.append(copy)
        return copy

    kept = []

    def local(src, dst, sem):
        copy = pltpu.make_async_copy(src, dst, sem)
        copy.start()
        kept.append(copy)

    load_geno = pltpu.make_async_copy(geno_hbm, geno, lsem.at[0])
    own_loads = []
    for c in range(chunks):
        own = pltpu.make_async_copy(est_hbm.at[pl.ds(c * rb, rb)], estbuf.at[c, me], lsem.at[1 + c])
        own.start()
        own_loads.append(own)

    barrier = pltpu.get_barrier_semaphore()
    peers = [partner] + [{"pp": xid(d)} for d in range(1, n_pp)] + [{"mk": zid(d)} for d in range(1, n_mk)]
    for peer in peers:
        pl.semaphore_signal(barrier, inc=1, device_id=peer, device_id_type=pl.DeviceIdType.MESH)
    pl.semaphore_wait(barrier, len(peers))

    copies = {}

    def gather_start(kind, c, src, buf, xs, xr, ps, pr):
        copies[kind, c, "x"] = [
            go(remote(src, buf.at[c, me], xs.at[c, d - 1], xr.at[c, d - 1], {"pp": xid(d)}))
            for d in range(1, n_pp)]
        copies[kind, c, "p"] = [go(remote(src, buf.at[c, me], ps.at[c, 0], pr.at[c, 0], partner))]

    def gather_forward(kind, c, buf, ps, pr):
        for d in range(1, n_pp):
            copies[kind, c, "x"][d - 1].wait_recv()
            origin = xback(d) * 2 + s
            copies[kind, c, "p"].append(
                go(remote(buf.at[c, origin], buf.at[c, origin], ps.at[c, d], pr.at[c, d], partner)))

    def gather_finish(kind, c):
        for copy in copies[kind, c, "p"]:
            copy.wait_recv()

    slab, noise = column(slab_ref[...]), column(noise_ref[...])
    spread = slab + noise
    base = column(prior_ref[...]) + 0.5 * jnp.log(noise / spread)
    curve = 1.0 / noise - 1.0 / spread
    shrink = slab / spread

    first = tc_ref[z * tile_dev]
    member = [[jnp.where(tc_ref[z * tile_dev + t] == first + k, 1.0, 0.0).astype(F32)
               for t in range(tile_dev)] for k in range(SPAN)]

    def a0(c):
        gather_start("a", c, est_hbm.at[pl.ds(c * rb, rb)], estbuf, ax_s, ax_r, ap_s, ap_r)

    def a1(c):
        gather_forward("a", c, estbuf, ap_s, ap_r)

    def a2(c):
        if c == 0:
            load_geno.wait()
        own_loads[c].wait()
        gather_finish("a", c)
        pred = lax.dot_general(estbuf[c].reshape(n_sh * rb, marks), geno[...], NT,
                               preferred_element_type=F32)
        pown[c] = pred.reshape(n_mk, g, people)
        pbuf[c] = pred.astype(BF16).reshape(n_mk, g, people)
        copies["b", c] = [
            go(remote(pbuf.at[c, zid(d)], precv.at[c, d - 1], bz_s.at[c, d - 1], bz_r.at[c, d - 1], {"mk": zid(d)}))
            for d in range(1, n_mk)]

    def phen_rows(c):
        return phen_ref[pl.ds(pl.multiple_of(z * share + c * g, g), g), :].astype(F32)

    def b1(c):
        total = pown[c, z]
        for d in range(1, n_mk):
            copies["b", c][d - 1].wait_recv()
            total = total + precv[c, d - 1].astype(F32)
        rbuf[c, z] = (phen_rows(c) - total).astype(BF16)
        copies["r", c] = [
            go(remote(rbuf.at[c, z], rbuf.at[c, z], rz_s.at[c, d - 1], rz_r.at[c, d - 1], {"mk": zid(d)}))
            for d in range(1, n_mk)]

    def b2(c):
        for copy in copies["r", c]:
            copy.wait_recv()
        residual = rbuf[c].reshape(n_sh * rb, people)
        for j in range(marks // TILE):
            cols = pl.ds(j * TILE, TILE)
            sbuf[c, :, :, cols] = jnp.dot(residual, geno[:, cols], preferred_element_type=F32).reshape(n_sh, rb, TILE)
        for q in range(n_pp):
            c1send[c, q] = sbuf[c, q * 2 + other].astype(BF16)
        copies["c1", c] = go(remote(c1send.at[c], c1recv.at[c], c1_s.at[c], c1_r.at[c], partner))

    def c2(c):
        copies["c1", c].wait_recv()
        copies["c2", c] = []
        for d in range(1, n_pp):
            q = xid(d)
            c2send[c, d - 1] = (sbuf[c, q * 2 + s] + c1recv[c, q].astype(F32)).astype(BF16)
            copies["c2", c].append(
                go(remote(c2send.at[c, d - 1], c2recv.at[c, d - 1], c2_s.at[c, d - 1], c2_r.at[c, d - 1], {"pp": q})))

    def c3(c):
        for copy in copies["c2", c]:
            copy.wait_recv()
        at = slice(c * rb, (c + 1) * rb)
        scores = sbuf[c, me] + c1recv[c, x].astype(F32)
        for d in range(1, n_pp):
            scores = scores + c2recv[c, d - 1].astype(F32)
        observed = marker_root * estbuf[c, me].astype(F32) + scores * (1.0 / people_root)
        log_odds = base[at] + 0.5 * observed * observed * curve[at]
        posterior = jax.nn.sigmoid(log_odds) * shrink[at] * observed
        new = (posterior * (1.0 / marker_root)).astype(BF16)
        ubuf[c, me] = new
        gather_start("d", c, ubuf.at[c, me], ubuf, dx_s, dx_r, dp_s, dp_r)
        local(ubuf.at[c, me], upd_hbm.at[pl.ds(c * rb, rb)], osem.at[c])

    def d1(c):
        gather_forward("d", c, ubuf, dp_s, dp_r)

    def d2(c):
        gather_finish("d", c)
        for t in range(tile_dev):
            cols = pl.ds(t * TILE, TILE)
            tbuf[t] = lax.dot_general(ubuf[c, :, :, cols].reshape(n_sh * rb, TILE), geno[:, cols], NT,
                                      preferred_element_type=F32).reshape(n_mk, g, people)
        for b in range(n_mk):
            for k in range(SPAN):
                acc = tbuf[0, b] * member[k][0]
                for t in range(1, tile_dev):
                    acc = acc + tbuf[t, b] * member[k][t]
                ebuf[c, b, k] = acc.astype(BF16)
        copies["e", c] = [
            go(remote(ebuf.at[c, zid(d)], slots_hbm.at[z, :, pl.ds(c * g, g)], ez_s.at[c, d - 1], ez_r.at[c, d - 1], {"mk": zid(d)}))
            for d in range(1, n_mk)]
        local(ebuf.at[c, z], slots_hbm.at[z, :, pl.ds(c * g, g)], ksem.at[c])

    def e1(c):
        for copy in copies["e", c]:
            copy.wait_recv()

    stages = [a1, a2, b1, b2, c2, c3, d1, d2, e1]
    for c in range(chunks):
        a0(c)
    load_geno.start()
    for names in (ORDER if chunks == 4 else [[k * 10 for k in range(len(stages))]]):
        for name in names:
            stages[name // 10](name % 10)
    for copy in started:
        copy.wait_send()
    for copy in kept:
        copy.wait()


def finish(dims, tc_ref, slots_ref, upd_ref, phen_ref, new_ref, loco_ref):
    n_mk, share, g, tile_dev = dims
    step = pl.program_id(0)
    new_ref[...] = upd_ref[...]
    at = pl.multiple_of(lax.axis_index("mk") * share + step * g, g)
    total = jnp.zeros(loco_ref.shape[1:], F32)
    for j in range(n_mk):
        for k in range(SPAN):
            total = total + slots_ref[j, k].astype(F32)
    rest = phen_ref[pl.ds(at, g), :].astype(F32) - total
    for q in range(CHROMS):
        value = rest
        for j in range(n_mk):
            slot = q - tc_ref[j * tile_dev]
            held = jnp.where((slot >= 0) & (slot < SPAN), 1.0, 0.0).astype(F32)
            value = value + slots_ref[j, jnp.clip(slot, 0, SPAN - 1)].astype(F32) * held
        loco_ref[q] = value.astype(BF16)


def per_device(genotypes, estimate, phenotypes, prior_logit, slab_var, noise_var, tile_chrom):
    people, marks = genotypes.shape
    n_mk, n_pp, n_sub = lax.axis_size("mk"), lax.axis_size("pp"), lax.axis_size("sub")
    traits, rows = phenotypes.shape[0], estimate.shape[0]
    share = traits // n_mk
    assert n_sub == 2
    chunks = CHUNKS if share == rows and rows % (16 * CHUNKS) == 0 else 1
    rb, g = rows // chunks, share // chunks
    n_sh, tile_dev = n_pp * 2, marks // TILE
    dims = (n_mk, n_pp, chunks, rows, rb, share, g, people, marks,
            math.sqrt(marks * n_mk), math.sqrt(people * n_pp * n_sub))
    vmem, dma = pltpu.VMEM, pltpu.SemaphoreType.DMA
    xs, zs = n_pp - 1, n_mk - 1
    in_vmem = pl.BlockSpec(memory_space=pltpu.VMEM)
    in_any = pl.BlockSpec(memory_space=pl.ANY)
    new, slots = pl.pallas_call(
        functools.partial(kernel, dims),
        out_shape=(jax.ShapeDtypeStruct((rows, marks), BF16),
                   jax.ShapeDtypeStruct((n_mk, SPAN, share, people), BF16)),
        in_specs=[pl.BlockSpec(memory_space=pltpu.SMEM), in_any, in_any, in_vmem, in_vmem, in_vmem, in_vmem],
        out_specs=(in_any, in_any),
        scratch_shapes=[
            vmem((people, marks), BF16),
            vmem((chunks, n_sh, rb, marks), BF16),
            vmem((chunks, n_mk, g, people), F32),
            vmem((chunks, n_mk, g, people), BF16),
            vmem((chunks, zs, g, people), BF16),
            vmem((chunks, n_mk, g, people), BF16),
            vmem((chunks, n_sh, rb, marks), F32),
            vmem((chunks, n_pp, rb, marks), BF16),
            vmem((chunks, n_pp, rb, marks), BF16),
            vmem((chunks, xs, rb, marks), BF16),
            vmem((chunks, xs, rb, marks), BF16),
            vmem((chunks, n_sh, rb, marks), BF16),
            vmem((tile_dev, n_mk, g, people), F32),
            vmem((chunks, n_mk, SPAN, g, people), BF16),
            dma((1 + chunks,)), dma((chunks,)), dma((chunks,)),
            dma((chunks, xs)), dma((chunks, xs)), dma((chunks, n_pp)), dma((chunks, n_pp)),
            dma((chunks, zs)), dma((chunks, zs)), dma((chunks, zs)), dma((chunks, zs)),
            dma((chunks,)), dma((chunks,)), dma((chunks, xs)), dma((chunks, xs)),
            dma((chunks, xs)), dma((chunks, xs)), dma((chunks, n_pp)), dma((chunks, n_pp)),
            dma((chunks, zs)), dma((chunks, zs)),
        ],
        compiler_params=pltpu.CompilerParams(
            collective_id=0, has_side_effects=True, vmem_limit_bytes=56 * 1024 * 1024),
    )(tile_chrom, genotypes, estimate, phenotypes,
      prior_logit.reshape(1, rows), slab_var.reshape(1, rows), noise_var.reshape(1, rows))
    return pl.pallas_call(
        functools.partial(finish, (n_mk, share, g, tile_dev)),
        grid=(chunks,),
        out_shape=(jax.ShapeDtypeStruct((rows, marks), BF16),
                   jax.ShapeDtypeStruct((CHROMS, share, people), BF16)),
        in_specs=[pl.BlockSpec(memory_space=pltpu.SMEM),
                  pl.BlockSpec((n_mk, SPAN, g, people), lambda i: (0, 0, i, 0)),
                  pl.BlockSpec((rb, marks), lambda i: (i, 0)),
                  pl.BlockSpec((traits, people), lambda i: (0, 0))],
        out_specs=(pl.BlockSpec((rb, marks), lambda i: (i, 0)),
                   pl.BlockSpec((CHROMS, g, people), lambda i: (0, i, 0))),
    )(tile_chrom, slots, new, phenotypes)


def solution(mesh):
    placed = (
        P(("grp", "pp", "sub"), "mk"),
        P(("grp", "pp", "sub"), "mk"),
        P("grp", ("pp", "sub")),
        P(("grp", "pp", "sub")),
        P(("grp", "pp", "sub")),
        P(("grp", "pp", "sub")),
        P("grp"),
    )
    return jax.shard_map(
        per_device,
        mesh=mesh,
        in_specs=placed,
        out_specs=(P(("grp", "pp", "sub"), "mk"), P("grp", "mk", ("pp", "sub"))),
        check_vma=False,
    )
```

```python
import functools
import math

import jax
import jax.numpy as jnp
from jax import lax
from jax.experimental import pallas as pl
from jax.experimental.pallas import tpu as pltpu
from jax.sharding import PartitionSpec as P

CHROMS = 22
TILE = 512
SPAN = 6
CHUNKS = 4
ORDER = [
    [0, 10, 1, 11, 2, 20, 12, 3, 21, 13, 30, 22, 31, 40, 23, 41, 32, 50],
    [42, 33, 51, 43, 60, 70, 52, 61, 71, 53, 62, 72, 63, 73, 80, 81, 82, 83],
]
F32 = jnp.float32
BF16 = jnp.bfloat16
NT = (((1,), (1,)), ((), ()))


def column(row):
    n = row.shape[1]
    at = lax.broadcasted_iota(jnp.int32, (n, n), 0)
    to = lax.broadcasted_iota(jnp.int32, (n, n), 1)
    return jnp.sum(jnp.where(at == to, jnp.broadcast_to(row, (n, n)), 0.0), axis=1, keepdims=True)


def kernel(dims, tc_ref, geno_hbm, est_hbm, phen_ref, prior_ref, slab_ref, noise_ref,
           upd_hbm, slots_hbm,
           geno, estbuf, pown, pbuf, precv, rbuf, sbuf, c1send, c1recv, c2send, c2recv,
           ubuf, tbuf, ebuf,
           lsem, osem, ksem, ax_s, ax_r, ap_s, ap_r, bz_s, bz_r, rz_s, rz_r, c1_s, c1_r, c2_s, c2_r,
           dx_s, dx_r, dp_s, dp_r, ez_s, ez_r):
    n_mk, n_pp, chunks, rows, rb, share, g, people, marks, marker_root, people_root = dims
    n_sh = n_pp * 2
    tile_dev = marks // TILE
    x, s, z = lax.axis_index("pp"), lax.axis_index("sub"), lax.axis_index("mk")
    other = 1 - s
    me = x * 2 + s
    partner = {"sub": other}

    def xid(d):
        return lax.rem(x + d, n_pp)

    def xback(d):
        return lax.rem(x + n_pp - d, n_pp)

    def zid(d):
        return lax.rem(z + d, n_mk)

    def remote(src, dst, send, recv, where):
        return pltpu.make_async_remote_copy(
            src_ref=src, dst_ref=dst, send_sem=send, recv_sem=recv,
            device_id=where, device_id_type=pl.DeviceIdType.MESH)

    started = []

    def go(copy):
        copy.start()
        started.append(copy)
        return copy

    kept = []

    def local(src, dst, sem):
        copy = pltpu.make_async_copy(src, dst, sem)
        copy.start()
        kept.append(copy)

    load_geno = pltpu.make_async_copy(geno_hbm, geno, lsem.at[0])
    own_loads = []
    for c in range(chunks):
        own = pltpu.make_async_copy(est_hbm.at[pl.ds(c * rb, rb)], estbuf.at[c, me], lsem.at[1 + c])
        own.start()
        own_loads.append(own)

    barrier = pltpu.get_barrier_semaphore()
    peers = [partner] + [{"pp": xid(d)} for d in range(1, n_pp)] + [{"mk": zid(d)} for d in range(1, n_mk)]
    for peer in peers:
        pl.semaphore_signal(barrier, inc=1, device_id=peer, device_id_type=pl.DeviceIdType.MESH)
    pl.semaphore_wait(barrier, len(peers))

    copies = {}

    def gather_start(kind, c, src, buf, xs, xr, ps, pr):
        copies[kind, c, "x"] = [
            go(remote(src, buf.at[c, me], xs.at[c, d - 1], xr.at[c, d - 1], {"pp": xid(d)}))
            for d in range(1, n_pp)]
        copies[kind, c, "p"] = [go(remote(src, buf.at[c, me], ps.at[c, 0], pr.at[c, 0], partner))]

    def gather_forward(kind, c, buf, ps, pr):
        for d in range(1, n_pp):
            copies[kind, c, "x"][d - 1].wait_recv()
            origin = xback(d) * 2 + s
            copies[kind, c, "p"].append(
                go(remote(buf.at[c, origin], buf.at[c, origin], ps.at[c, d], pr.at[c, d], partner)))

    def gather_finish(kind, c):
        for copy in copies[kind, c, "p"]:
            copy.wait_recv()

    slab, noise = column(slab_ref[...]), column(noise_ref[...])
    spread = slab + noise
    base = column(prior_ref[...]) + 0.5 * jnp.log(noise / spread)
    curve = 1.0 / noise - 1.0 / spread
    shrink = slab / spread

    first = tc_ref[z * tile_dev]
    member = [[jnp.where(tc_ref[z * tile_dev + t] == first + k, 1.0, 0.0).astype(F32)
               for t in range(tile_dev)] for k in range(SPAN)]

    def a0(c):
        gather_start("a", c, est_hbm.at[pl.ds(c * rb, rb)], estbuf, ax_s, ax_r, ap_s, ap_r)

    def a1(c):
        gather_forward("a", c, estbuf, ap_s, ap_r)

    def a2(c):
        if c == 0:
            load_geno.wait()
        own_loads[c].wait()
        gather_finish("a", c)
        pred = lax.dot_general(estbuf[c].reshape(n_sh * rb, marks), geno[...], NT,
                               preferred_element_type=F32)
        pown[c] = pred.reshape(n_mk, g, people)
        pbuf[c] = pred.astype(BF16).reshape(n_mk, g, people)
        copies["b", c] = [
            go(remote(pbuf.at[c, zid(d)], precv.at[c, d - 1], bz_s.at[c, d - 1], bz_r.at[c, d - 1], {"mk": zid(d)}))
            for d in range(1, n_mk)]

    def phen_rows(c):
        return phen_ref[pl.ds(pl.multiple_of(z * share + c * g, g), g), :].astype(F32)

    def b1(c):
        total = pown[c, z]
        for d in range(1, n_mk):
            copies["b", c][d - 1].wait_recv()
            total = total + precv[c, d - 1].astype(F32)
        rbuf[c, z] = (phen_rows(c) - total).astype(BF16)
        copies["r", c] = [
            go(remote(rbuf.at[c, z], rbuf.at[c, z], rz_s.at[c, d - 1], rz_r.at[c, d - 1], {"mk": zid(d)}))
            for d in range(1, n_mk)]

    def b2(c):
        for copy in copies["r", c]:
            copy.wait_recv()
        residual = rbuf[c].reshape(n_sh * rb, people)
        for j in range(marks // TILE):
            cols = pl.ds(j * TILE, TILE)
            sbuf[c, :, :, cols] = jnp.dot(residual, geno[:, cols], preferred_element_type=F32).reshape(n_sh, rb, TILE)
        for q in range(n_pp):
            c1send[c, q] = sbuf[c, q * 2 + other].astype(BF16)
        copies["c1", c] = go(remote(c1send.at[c], c1recv.at[c], c1_s.at[c], c1_r.at[c], partner))

    def c2(c):
        copies["c1", c].wait_recv()
        copies["c2", c] = []
        for d in range(1, n_pp):
            q = xid(d)
            c2send[c, d - 1] = (sbuf[c, q * 2 + s] + c1recv[c, q].astype(F32)).astype(BF16)
            copies["c2", c].append(
                go(remote(c2send.at[c, d - 1], c2recv.at[c, d - 1], c2_s.at[c, d - 1], c2_r.at[c, d - 1], {"pp": q})))

    def c3(c):
        for copy in copies["c2", c]:
            copy.wait_recv()
        at = slice(c * rb, (c + 1) * rb)
        scores = sbuf[c, me] + c1recv[c, x].astype(F32)
        for d in range(1, n_pp):
            scores = scores + c2recv[c, d - 1].astype(F32)
        observed = marker_root * estbuf[c, me].astype(F32) + scores * (1.0 / people_root)
        log_odds = base[at] + 0.5 * observed * observed * curve[at]
        posterior = jax.nn.sigmoid(log_odds) * shrink[at] * observed
        new = (posterior * (1.0 / marker_root)).astype(BF16)
        ubuf[c, me] = new
        gather_start("d", c, ubuf.at[c, me], ubuf, dx_s, dx_r, dp_s, dp_r)
        local(ubuf.at[c, me], upd_hbm.at[pl.ds(c * rb, rb)], osem.at[c])

    def d1(c):
        gather_forward("d", c, ubuf, dp_s, dp_r)

    def d2(c):
        gather_finish("d", c)
        for t in range(tile_dev):
            cols = pl.ds(t * TILE, TILE)
            tbuf[t] = lax.dot_general(ubuf[c, :, :, cols].reshape(n_sh * rb, TILE), geno[:, cols], NT,
                                      preferred_element_type=F32).reshape(n_mk, g, people)
        for b in range(n_mk):
            for k in range(SPAN):
                acc = tbuf[0, b] * member[k][0]
                for t in range(1, tile_dev):
                    acc = acc + tbuf[t, b] * member[k][t]
                ebuf[c, b, k] = acc.astype(BF16)
        copies["e", c] = [
            go(remote(ebuf.at[c, zid(d)], slots_hbm.at[z, :, pl.ds(c * g, g)], ez_s.at[c, d - 1], ez_r.at[c, d - 1], {"mk": zid(d)}))
            for d in range(1, n_mk)]
        local(ebuf.at[c, z], slots_hbm.at[z, :, pl.ds(c * g, g)], ksem.at[c])

    def e1(c):
        for copy in copies["e", c]:
            copy.wait_recv()

    stages = [a1, a2, b1, b2, c2, c3, d1, d2, e1]
    for c in range(chunks):
        a0(c)
    load_geno.start()
    for names in (ORDER if chunks == 4 else [[k * 10 for k in range(len(stages))]]):
        for name in names:
            stages[name // 10](name % 10)
    for copy in started:
        copy.wait_send()
    for copy in kept:
        copy.wait()


def finish(dims, tc_ref, slots_ref, upd_ref, phen_ref, new_ref, loco_ref):
    n_mk, share, g, tile_dev = dims
    step = pl.program_id(0)
    new_ref[...] = upd_ref[...]
    at = pl.multiple_of(lax.axis_index("mk") * share + step * g, g)
    total = jnp.zeros(loco_ref.shape[1:], F32)
    for j in range(n_mk):
        for k in range(SPAN):
            total = total + slots_ref[j, k].astype(F32)
    rest = phen_ref[pl.ds(at, g), :].astype(F32) - total
    for q in range(CHROMS):
        value = rest
        for j in range(n_mk):
            slot = q - tc_ref[j * tile_dev]
            held = jnp.where((slot >= 0) & (slot < SPAN), 1.0, 0.0).astype(F32)
            value = value + slots_ref[j, jnp.clip(slot, 0, SPAN - 1)].astype(F32) * held
        loco_ref[q] = value.astype(BF16)


def per_device(genotypes, estimate, phenotypes, prior_logit, slab_var, noise_var, tile_chrom):
    people, marks = genotypes.shape
    n_mk, n_pp, n_sub = lax.axis_size("mk"), lax.axis_size("pp"), lax.axis_size("sub")
    traits, rows = phenotypes.shape[0], estimate.shape[0]
    share = traits // n_mk
    assert n_sub == 2
    chunks = CHUNKS if share == rows and rows % (16 * CHUNKS) == 0 else 1
    rb, g = rows // chunks, share // chunks
    n_sh, tile_dev = n_pp * 2, marks // TILE
    dims = (n_mk, n_pp, chunks, rows, rb, share, g, people, marks,
            math.sqrt(marks * n_mk), math.sqrt(people * n_pp * n_sub))
    vmem, dma = pltpu.VMEM, pltpu.SemaphoreType.DMA
    xs, zs = n_pp - 1, n_mk - 1
    in_vmem = pl.BlockSpec(memory_space=pltpu.VMEM)
    in_any = pl.BlockSpec(memory_space=pl.ANY)
    new, slots = pl.pallas_call(
        functools.partial(kernel, dims),
        out_shape=(jax.ShapeDtypeStruct((rows, marks), BF16),
                   jax.ShapeDtypeStruct((n_mk, SPAN, share, people), BF16)),
        in_specs=[pl.BlockSpec(memory_space=pltpu.SMEM), in_any, in_any, in_vmem, in_vmem, in_vmem, in_vmem],
        out_specs=(in_any, in_any),
        scratch_shapes=[
            vmem((people, marks), BF16),
            vmem((chunks, n_sh, rb, marks), BF16),
            vmem((chunks, n_mk, g, people), F32),
            vmem((chunks, n_mk, g, people), BF16),
            vmem((chunks, zs, g, people), BF16),
            vmem((chunks, n_mk, g, people), BF16),
            vmem((chunks, n_sh, rb, marks), F32),
            vmem((chunks, n_pp, rb, marks), BF16),
            vmem((chunks, n_pp, rb, marks), BF16),
            vmem((chunks, xs, rb, marks), BF16),
            vmem((chunks, xs, rb, marks), BF16),
            vmem((chunks, n_sh, rb, marks), BF16),
            vmem((tile_dev, n_mk, g, people), F32),
            vmem((chunks, n_mk, SPAN, g, people), BF16),
            dma((1 + chunks,)), dma((chunks,)), dma((chunks,)),
            dma((chunks, xs)), dma((chunks, xs)), dma((chunks, n_pp)), dma((chunks, n_pp)),
            dma((chunks, zs)), dma((chunks, zs)), dma((chunks, zs)), dma((chunks, zs)),
            dma((chunks,)), dma((chunks,)), dma((chunks, xs)), dma((chunks, xs)),
            dma((chunks, xs)), dma((chunks, xs)), dma((chunks, n_pp)), dma((chunks, n_pp)),
            dma((chunks, zs)), dma((chunks, zs)),
        ],
        compiler_params=pltpu.CompilerParams(
            collective_id=0, has_side_effects=True, vmem_limit_bytes=56 * 1024 * 1024),
    )(tile_chrom, genotypes, estimate, phenotypes,
      prior_logit.reshape(1, rows), slab_var.reshape(1, rows), noise_var.reshape(1, rows))
    return pl.pallas_call(
        functools.partial(finish, (n_mk, share, g, tile_dev)),
        grid=(chunks,),
        out_shape=(jax.ShapeDtypeStruct((rows, marks), BF16),
                   jax.ShapeDtypeStruct((CHROMS, share, people), BF16)),
        in_specs=[pl.BlockSpec(memory_space=pltpu.SMEM),
                  pl.BlockSpec((n_mk, SPAN, g, people), lambda i: (0, 0, i, 0)),
                  pl.BlockSpec((rb, marks), lambda i: (i, 0)),
                  pl.BlockSpec((traits, people), lambda i: (0, 0))],
        out_specs=(pl.BlockSpec((rb, marks), lambda i: (i, 0)),
                   pl.BlockSpec((CHROMS, g, people), lambda i: (0, i, 0))),
    )(tile_chrom, slots, new, phenotypes)


def solution(mesh):
    placed = (
        P(("grp", "pp", "sub"), "mk"),
        P(("grp", "pp", "sub"), "mk"),
        P("grp", ("pp", "sub")),
        P(("grp", "pp", "sub")),
        P(("grp", "pp", "sub")),
        P(("grp", "pp", "sub")),
        P("grp"),
    )
    return jax.shard_map(
        per_device,
        mesh=mesh,
        in_specs=placed,
        out_specs=(P(("grp", "pp", "sub"), "mk"), P("grp", "mk", ("pp", "sub"))),
        check_vma=False,
    )
```
